32 devices in a mesh: row: 4 (over z), col: 8 (over y, x, core).
Axes of the slice: x: 2, y: 2, z: 4, core: 2. Of those that a mesh axis runs over, the one named last changes fastest.
Arguments:
- tokens: bfloat16 [8192, 2048], P('row', 'col'), may hold values from -6 to 6
- doc_ids: int32 [8192], P('row'), may hold values from 0 to 15, never falling along the last dimension, each value on 1 to 1024 neighbouring positions
- norm1_gain: bfloat16 [2048], P('col'), may hold values from 0.5 to 1.5
- norm1_bias: bfloat16 [2048], P('col'), may hold values from -1.796875 to 1.796875
- norm2_gain: bfloat16 [2048], P('col'), may hold values from 0.5 to 1.5
- norm2_bias: bfloat16 [2048], P('col'), may hold values from -1.796875 to 1.796875
- w_qkv: bfloat16 [2048, 16, 384], P('row', 'col'), may hold values from -0.125 to 0.125
- b_qkv: bfloat16 [16, 384], P('col'), may hold values from -1.796875 to 1.796875
- w_out: bfloat16 [2048, 2048], P('col', 'row'), may hold values from -0.5 to 0.5
- b_out: bfloat16 [2048], P('row'), may hold values from -1.796875 to 1.796875
- w_up: bfloat16 [2048, 8192], P('row', 'col'), may hold values from -0.125 to 0.125
- b_up: bfloat16 [8192], P('col'), may hold values from -1.796875 to 1.796875
- w_down: bfloat16 [8192, 2048], P('col', 'row'), may hold values from -0.0625 to 0.0625
- b_down: bfloat16 [2048], P('row'), may hold values from -1.796875 to 1.796875
- cotangent: bfloat16 [8192, 2048], P('row', 'col'), may hold values from -6 to 6
Outputs:
- layer_out: bfloat16 [8192, 2048], P('row', 'col')
- grad_tokens: float32 [8192, 2048], P('row', 'col')
- grad_norm1_gain: float32 [2048], P('col')
- grad_norm1_bias: float32 [2048], P('col')
- grad_norm2_gain: float32 [2048], P('col')
- grad_norm2_bias: float32 [2048], P('col')
- grad_w_qkv: float32 [2048, 16, 384], P('row', 'col')
- grad_b_qkv: float32 [16, 384], P('col')
- grad_w_out: float32 [2048, 2048], P('col', 'row')
- grad_b_out: float32 [2048], P('row')
- grad_w_up: float32 [2048, 8192], P('row', 'col')
- grad_b_up: float32 [8192], P('col')
- grad_w_down: float32 [8192, 2048], P('col', 'row')
- grad_b_down: float32 [2048], P('row')
The draws below stay inside these ranges and needn't reach their ends.
Inputs may be any that keep to these rules, and one draw needn't show every extreme that they name: `doc_ids`: document numbers never fall along the tokens.
All inputs are finite; a program needn't handle non-finite values.
Results may differ from the reference program's by a relative error of at most 0.0095.
Values may be sent and summed in bfloat16 or wider, within the bound.
No kernel may reach another device: no remote copies, remote signals or barrier semaphores. Data moves between devices by JAX's collectives and lax.ppermute only.
A program may use at most 256 MiB of HBM per device.

```python
import functools
import math
import jax
import jax.numpy as jnp
import numpy as np
from jax import lax

D = 2048
H = 16
HD = 128
ROT = 32
FF = 8192
TOK_ROW = 2048
TOKENS = 8192
N_ROW = 4


def steps_of(key, extent, shards, smallest, high):
    def one(position, parts):
        draws = jax.random.uniform(jax.random.fold_in(jax.random.fold_in(key, 6), position), (parts,), jnp.float32, smallest / len(shards), high / len(shards))
        return jnp.repeat(jnp.exp(draws), extent[position] // parts).reshape((-1,) + (1,) * (len(extent) - position - 1))

    level = one(*shards[0])
    for cut in shards[1:]:
        level = level * one(*cut)
    return level


def profile(count, total, most, slope):
    portions = [(1 << 20) // math.isqrt(rank ** slope) + 1 for rank in range(2, count + 1)]
    spare, counts = total - most - (count - 1), [1] * (count - 1)
    while spare > 0:
        candidates = [i for i in range(count - 1) if counts[i] < most]
        mass, remaining = sum([portions[i] for i in candidates]), spare
        for i in candidates:
            addition = min(most - counts[i], max(1, remaining * portions[i] // mass), spare)
            counts[i] = counts[i] + addition
            spare = spare - addition
    return np.array([most] + counts)


def uneven(rng, amount, total, reach, slope):
    if amount == 2:
        one = jax.random.randint(rng, (), max(1, total - reach), min(reach, total - 1) + 1)
        return jnp.stack([one, total - one])
    tallies = jnp.asarray(profile(amount, total, reach, slope), jnp.int32)
    couples = (amount - 1) // 2
    donor, sink = tallies[1:1 + 2 * couples:2], tallies[2:2 + 2 * couples:2]
    room = jnp.minimum(donor - 1, reach - sink)
    passed = jax.random.randint(jax.random.fold_in(rng, 1), (couples,), 0, 1 << 20) % (room + 1)
    tallies = tallies.at[1:1 + 2 * couples:2].set(donor - passed).at[2:2 + 2 * couples:2].set(sink + passed)
    return tallies[jax.random.permutation(jax.random.fold_in(rng, 2), amount)]


def bell_draw(stream_key, dims, width, limit, cuts=(), kind=jnp.bfloat16):
    values = jax.random.normal(stream_key, dims, jnp.float32) * width
    if len(cuts) > 0:
        values = steps_of(stream_key, dims, cuts, -0.22, 0.18) * values
    return jnp.clip(values, min=-limit, max=limit).astype(kind)


def setup_inputs(seed: int = 0) -> dict:
    keys = jax.random.split(jax.random.key(seed), 16)
    return {
        "tokens": bell_draw(keys[0], (TOKENS, D), 1.0, 6.0, ((0, 4), (1, 8))),
        "doc_ids": jnp.searchsorted(jnp.cumsum(uneven(keys[1], TOKENS * 4 // TOK_ROW, TOKENS, TOK_ROW // 2, 2)), jnp.arange(TOKENS), side="right").astype(jnp.int32),
        "norm1_gain": jnp.clip(1.0 + 0.1 * jax.random.normal(keys[2], (D,), jnp.float32), 0.5, 1.5).astype(jnp.bfloat16),
        "norm1_bias": bell_draw(keys[3], (D,), 0.3, 1.796875, ((0, 8),)),
        "norm2_gain": jnp.clip(1.0 + 0.1 * jax.random.normal(keys[4], (D,), jnp.float32), 0.5, 1.5).astype(jnp.bfloat16),
        "norm2_bias": bell_draw(keys[5], (D,), 0.3, 1.796875, ((0, 8),)),
        "w_qkv": bell_draw(keys[6], (D, H, 3 * HD), D ** -0.5, 0.125, ((0, 4), (1, 8))),
        "b_qkv": bell_draw(keys[7], (H, 3 * HD), 0.3, 1.796875, ((0, 8),)),
        "w_out": bell_draw(keys[8], (D, D), (D // 16) ** -0.5, 0.5, ((0, 8), (1, 4))),
        "b_out": bell_draw(keys[9], (D,), 0.3, 1.796875, ((0, 4),)),
        "w_up": bell_draw(keys[10], (D, FF), D ** -0.5, 0.125, ((0, 4), (1, 8))),
        "b_up": bell_draw(keys[11], (FF,), 0.3, 1.796875, ((0, 8),)),
        "w_down": bell_draw(keys[12], (FF, D), FF ** -0.5, 0.0625, ((0, 8), (1, 4))),
        "b_down": bell_draw(keys[13], (D,), 0.3, 1.796875, ((0, 4),)),
        "cotangent": bell_draw(keys[14], (TOKENS, D), 1.0, 6.0, ((0, 4), (1, 8))),
    }


EPSILON = 1e-05
MASKED = -1e+30
ROPE_BASE = 10000.0
HIGHEST = lax.Precision.HIGHEST

@jax.custom_vjp
def low(v):
    return lax.optimization_barrier(v.astype(jnp.bfloat16)).astype(jnp.float32)

@jax.custom_vjp
def low_back(v):
    return v

def low_keep(v):
    return (low(v), None)

def low_pass(kept, grad):
    return (grad,)

def back_keep(v):
    return (v, None)

def back_low(kept, grad):
    return (low(grad),)
low.defvjp(low_keep, low_pass)
low_back.defvjp(back_keep, back_low)

def layer_norm(tokens_wide, gain, shift):
    row_mean = lax.optimization_barrier(jnp.mean(tokens_wide, axis=-1, keepdims=True))
    centered = tokens_wide - row_mean
    row_var = lax.optimization_barrier(jnp.mean(centered * centered, axis=-1, keepdims=True))
    return centered * lax.rsqrt(row_var + EPSILON) * gain + shift

def positions(doc_ids):
    length = doc_ids.shape[0]
    places = jnp.arange(length, dtype=jnp.int32)
    change = jnp.concatenate([jnp.ones((1,), dtype=jnp.bool_), doc_ids[1:] != doc_ids[:-1]])
    starts = lax.cummax(jnp.where(change, places, 0).astype(jnp.int32), axis=0)
    return places - starts

def rotary_tables(places):
    exponent = jnp.arange(0, ROT, 2, dtype=jnp.float32) / ROT
    inverse = 1.0 / ROPE_BASE ** exponent
    angles = places.astype(jnp.float32)[:, None] * inverse[None, :]
    angles = jnp.concatenate([angles, angles], axis=1)
    return (jnp.cos(angles), jnp.sin(angles))

def rotate(field, cos_table, sin_table):
    half_rot = ROT // 2
    turned_part = field[..., :ROT]
    turned = jnp.concatenate([-turned_part[..., half_rot:], turned_part[..., :half_rot]], axis=-1)
    return jnp.concatenate([turned_part * cos_table + turned * sin_table, field[..., ROT:]], axis=-1)

def attend_head(paired):
    joint_head, doc_ids = paired
    cos_table, sin_table = rotary_tables(positions(doc_ids))
    queries = low(rotate(joint_head[:, :HD], cos_table, sin_table))
    keys_low = low(rotate(joint_head[:, HD:2 * HD], cos_table, sin_table))
    values = low(joint_head[:, 2 * HD:])
    scores = jnp.dot(queries, keys_low.T, precision=HIGHEST, preferred_element_type=jnp.float32)
    scores = low_back(scores * (1.0 / math.sqrt(HD)))
    places = jnp.arange(TOK_ROW, dtype=jnp.int32)
    allowed = (places[None, :] <= places[:, None]) & (doc_ids[None, :] == doc_ids[:, None])
    scores = jnp.where(allowed, scores, MASKED)
    row_peak = lax.optimization_barrier(jnp.max(scores, axis=-1, keepdims=True))
    log_total = row_peak + jnp.log(lax.optimization_barrier(jnp.sum(jnp.exp(scores - row_peak), axis=-1, keepdims=True)))
    probs_low = low(jnp.exp(scores - log_total))
    return jnp.dot(probs_low, values, precision=HIGHEST, preferred_element_type=jnp.float32)

def forward(tokens, norm1_gain, norm1_bias, norm2_gain, norm2_bias, w_qkv, b_qkv, w_out, b_out, w_up, b_up, w_down, b_down, doc_ids):
    h_first = low(layer_norm(tokens, norm1_gain, norm1_bias))
    h_second = low(layer_norm(tokens, norm2_gain, norm2_bias))
    qkv_joint = jnp.dot(h_first, w_qkv.reshape(D, H * 3 * HD), precision=HIGHEST, preferred_element_type=jnp.float32)
    qkv_joint = low_back(qkv_joint + b_qkv.reshape(H * 3 * HD))
    per_head = qkv_joint.reshape(N_ROW, TOK_ROW, H, 3 * HD).transpose(0, 2, 1, 3).reshape(N_ROW * H, TOK_ROW, 3 * HD)
    docs_each = jnp.repeat(doc_ids.reshape(N_ROW, TOK_ROW), H, axis=0)
    attended = lax.map(jax.checkpoint(attend_head), (per_head, docs_each))
    attended = attended.reshape(N_ROW, H, TOK_ROW, HD).transpose(0, 2, 1, 3).reshape(TOKENS, D)
    attended = low(low_back(attended))
    pre_act = low_back(jnp.dot(h_second, w_up, precision=HIGHEST, preferred_element_type=jnp.float32) + b_up)
    gelu_low = low(jax.nn.gelu(pre_act, approximate=False))
    attn_branch = jnp.dot(attended, w_out, precision=HIGHEST, preferred_element_type=jnp.float32) + b_out
    mlp_branch = jnp.dot(gelu_low, w_down, precision=HIGHEST, preferred_element_type=jnp.float32) + b_down
    return tokens + attn_branch + mlp_branch

def reference(tokens, doc_ids, norm1_gain, norm1_bias, norm2_gain, norm2_bias, w_qkv, b_qkv, w_out, b_out, w_up, b_up, w_down, b_down, cotangent):
    closed = functools.partial(forward, doc_ids=doc_ids)
    result, pullback = jax.vjp(closed, tokens.astype(jnp.float32), norm1_gain.astype(jnp.float32), norm1_bias.astype(jnp.float32), norm2_gain.astype(jnp.float32), norm2_bias.astype(jnp.float32), w_qkv.astype(jnp.float32), b_qkv.astype(jnp.float32), w_out.astype(jnp.float32), b_out.astype(jnp.float32), w_up.astype(jnp.float32), b_up.astype(jnp.float32), w_down.astype(jnp.float32), b_down.astype(jnp.float32))
    grads = pullback(cotangent.astype(jnp.float32))
    return (result.astype(jnp.bfloat16), grads[0], grads[1], grads[2], grads[3], grads[4], grads[5], grads[6], grads[7], grads[8], grads[9], grads[10], grads[11], grads[12])
```

```python
import functools
import math

import jax
import jax.numpy as jnp
from jax import lax
from jax.experimental import pallas as pl
from jax.experimental.pallas import tpu as pltpu
from jax.sharding import PartitionSpec as P

ROT = 32
EPSILON = 1e-05
MASKED = -1e30
ROPE_BASE = 10000.0
DOC_MAX = 1024
NT = (((1,), (1,)), ((), ()))
TN = (((0,), (0,)), ((), ()))
F32 = jnp.float32
BF16 = jnp.bfloat16
VMEM_LIMIT = 56 * 1024 * 1024


def run_starts(doc_ids):
    places = jnp.arange(doc_ids.shape[0], dtype=jnp.int32)
    change = jnp.concatenate([jnp.ones((1,), dtype=jnp.bool_), doc_ids[1:] != doc_ids[:-1]])
    return lax.cummax(jnp.where(change, places, 0), axis=0)


def rotary_tables(places, head_dim):
    exponent = jnp.arange(0, ROT, 2, dtype=F32) / ROT
    inverse = 1.0 / ROPE_BASE**exponent
    angles = inverse[:, None] * places.astype(F32)[None, :]
    cos, sin = jnp.cos(angles).T, jnp.sin(angles).T
    rest = (places.shape[0], head_dim - ROT)
    return (
        jnp.concatenate([cos, cos, jnp.ones(rest, F32)], axis=1),
        jnp.concatenate([sin, sin, jnp.zeros(rest, F32)], axis=1),
    )


def turn(field, cos, sin):
    half = ROT // 2
    width = field.shape[1]
    lane = lax.broadcasted_iota(jnp.int32, field.shape, 1)
    swapped = jnp.where(
        lane < half, -pltpu.roll(field, width - half, 1), pltpu.roll(field, half, 1)
    )
    return field * cos + swapped * sin


def turn_back(field, cos, sin):
    half = ROT // 2
    width = field.shape[1]
    lane = lax.broadcasted_iota(jnp.int32, field.shape, 1)
    crossed = field * sin
    swapped = jnp.where(
        lane < half,
        pltpu.roll(crossed, width - half, 1),
        jnp.where(lane < ROT, -pltpu.roll(crossed, half, 1), 0.0),
    )
    return field * cos + swapped


def attention_body(
    block,
    most,
    scale,
    low_ref,
    start_ref,
    q_ref,
    k_ref,
    v_ref,
    grad_ref,
    cos_q_ref,
    sin_q_ref,
    cos_k_ref,
    sin_k_ref,
    out_ref,
    joint_ref,
    key_ref,
    key_t_ref,
    val_ref,
    val_t_ref,
    dk_ref,
    dv_ref,
):
    step = pl.program_id(1)
    head_dim = q_ref.shape[1]

    @pl.when(step == 0)
    def _():
        turned = turn(k_ref[...], cos_k_ref[...], sin_k_ref[...])
        key_ref[...] = turned.astype(BF16)
        key_t_ref[...] = turned.T.astype(BF16)
        val_ref[...] = v_ref[...].astype(BF16)
        val_t_ref[...] = v_ref[...].T.astype(BF16)
        dk_ref[...] = jnp.zeros_like(dk_ref)
        dv_ref[...] = jnp.zeros_like(dv_ref)

    cos_q = cos_q_ref[...]
    sin_q = sin_q_ref[...]
    low = low_ref[step]
    count = step - low + 1
    rows = pl.ds(pl.multiple_of(step * block, block), block)

    def attend(blocks):
        query = turn(q_ref[...], cos_q, sin_q).astype(BF16)
        grad = grad_ref[...]
        length = blocks * block
        first = pl.multiple_of(low * block, block)
        span = pl.ds(first, length)
        scores = lax.dot_general(key_ref[span, :], query, NT, preferred_element_type=F32) * scale
        key_place = first + lax.broadcasted_iota(jnp.int32, scores.shape, 0)
        query_place = step * block + lax.broadcasted_iota(jnp.int32, scores.shape, 1)
        allowed = (key_place <= query_place) & (key_place >= start_ref[...])
        scores = jnp.where(allowed, scores, MASKED)
        peak = jnp.max(scores, axis=0, keepdims=True)
        raised = jnp.exp(scores - peak)
        probs = raised * (1.0 / jnp.sum(raised, axis=0, keepdims=True))
        probs_low = probs.astype(BF16)
        attended = jnp.dot(val_t_ref[:, span], probs_low, preferred_element_type=F32)
        out_ref[...] = attended.T.astype(BF16)
        d_probs = lax.dot_general(val_ref[span, :], grad, NT, preferred_element_type=F32)
        delta = jnp.sum(probs * d_probs, axis=0, keepdims=True)
        d_scores = (probs * (d_probs - delta)).astype(BF16)
        d_query = jnp.dot(key_t_ref[:, span], d_scores, preferred_element_type=F32).T * scale
        joint_ref[rows, 0:head_dim] = turn_back(d_query, cos_q, sin_q).astype(BF16)
        dk_ref[span, :] += jnp.dot(d_scores, query, preferred_element_type=F32)
        dv_ref[span, :] += jnp.dot(probs_low, grad, preferred_element_type=F32)

    for blocks in range(1, most + 1):
        pl.when(count == blocks)(functools.partial(attend, blocks))

    @pl.when(step == pl.num_programs(1) - 1)
    def _():
        d_key = turn_back(dk_ref[...] * scale, cos_k_ref[...], sin_k_ref[...])
        joint_ref[:, head_dim : 2 * head_dim] = d_key.astype(BF16)
        joint_ref[:, 2 * head_dim :] = dv_ref[...].astype(BF16)


def attention(qkv, d_attn, starts, cos, sin, head_dim):
    length = qkv.shape[0]
    heads = qkv.shape[1] // (3 * head_dim)
    block = min(256, length)
    steps = length // block
    most = min(steps, DOC_MAX // block + 1)
    low = (starts[::block] // block).astype(jnp.int32)
    whole = lambda part: pl.BlockSpec((length, head_dim), lambda h, i, low: (0, 3 * h + part))
    tile = pl.BlockSpec((block, head_dim), lambda h, i, low: (i, h))
    table = pl.BlockSpec((block, head_dim), lambda h, i, low: (i, 0))
    full_table = pl.BlockSpec((length, head_dim), lambda h, i, low: (0, 0))
    return pl.pallas_call(
        functools.partial(attention_body, block, most, 1.0 / math.sqrt(head_dim)),
        out_shape=(
            jax.ShapeDtypeStruct((length, heads * head_dim), BF16),
            jax.ShapeDtypeStruct((length, heads * 3 * head_dim), BF16),
        ),
        grid_spec=pltpu.PrefetchScalarGridSpec(
            num_scalar_prefetch=1,
            grid=(heads, steps),
            in_specs=[
                pl.BlockSpec((1, block), lambda h, i, low: (0, i)),
                pl.BlockSpec((block, head_dim), lambda h, i, low: (i, 3 * h)),
                whole(1),
                whole(2),
                tile,
                table,
                table,
                full_table,
                full_table,
            ],
            out_specs=(
                tile,
                pl.BlockSpec((length, 3 * head_dim), lambda h, i, low: (0, h)),
            ),
            scratch_shapes=[
                pltpu.VMEM((length, head_dim), BF16),
                pltpu.VMEM((head_dim, length), BF16),
                pltpu.VMEM((length, head_dim), BF16),
                pltpu.VMEM((head_dim, length), BF16),
                pltpu.VMEM((length, head_dim), F32),
                pltpu.VMEM((length, head_dim), F32),
            ],
        ),
        compiler_params=pltpu.CompilerParams(
            dimension_semantics=("arbitrary", "arbitrary"), vmem_limit_bytes=VMEM_LIMIT
        ),
        cost_estimate=pl.CostEstimate(
            flops=heads * length * 3 * block * head_dim * 10,
            bytes_accessed=heads * length * head_dim * 24,
            transcendentals=heads * length * 3 * block,
        ),
        name="attention",
    )(low, starts[None, :], qkv, qkv, qkv, d_attn, cos, sin, cos, sin)


def norm_body(x_ref, affine_ref, one_ref, two_ref, stat_ref):
    x = x_ref[...].astype(F32)
    mean = jnp.mean(x, axis=1, keepdims=True)
    centered = x - mean
    scale = lax.rsqrt(jnp.mean(centered * centered, axis=1, keepdims=True) + EPSILON)
    normed = centered * scale
    affine = affine_ref[...].astype(F32)
    one_ref[...] = (normed * affine[0:1] + affine[1:2]).astype(BF16)
    two_ref[...] = (normed * affine[2:3] + affine[3:4]).astype(BF16)
    stat_ref[...] = jnp.concatenate([mean, scale], axis=1)


def normalize(x, affine):
    length, width = x.shape
    block = min(256, length)
    rows = pl.BlockSpec((block, width), lambda i: (i, 0))
    return pl.pallas_call(
        norm_body,
        out_shape=(
            jax.ShapeDtypeStruct((length, width), BF16),
            jax.ShapeDtypeStruct((length, width), BF16),
            jax.ShapeDtypeStruct((length, 2), F32),
        ),
        grid=(length // block,),
        in_specs=[rows, pl.BlockSpec(affine.shape, lambda i: (0, 0))],
        out_specs=(rows, rows, pl.BlockSpec((block, 2), lambda i: (i, 0))),
        compiler_params=pltpu.CompilerParams(vmem_limit_bytes=VMEM_LIMIT),
        cost_estimate=pl.CostEstimate(
            flops=10 * length * width, bytes_accessed=6 * length * width, transcendentals=length
        ),
        name="normalize",
    )(x, affine)


def gelu_slope(pre_act):
    normal_cdf = 0.5 * (1.0 + lax.erf(pre_act * (1.0 / math.sqrt(2.0))))
    density = jnp.exp(-0.5 * pre_act * pre_act) * (1.0 / math.sqrt(2.0 * math.pi))
    return pre_act * normal_cdf, normal_cdf + pre_act * density


def swap(offset, size):
    return [(i, i ^ offset) for i in range(size)]


def per_device(
    tokens,
    doc_ids,
    norm1_gain,
    norm1_bias,
    norm2_gain,
    norm2_bias,
    w_qkv,
    b_qkv,
    w_out,
    b_out,
    w_up,
    b_up,
    w_down,
    b_down,
    cotangent,
):
    seq_rows, width_dev = tokens.shape
    n_row = lax.axis_size("row")
    n_col = lax.axis_size("col")
    width = width_dev * n_col
    rows_dev, heads_dev, triple = w_qkv.shape
    head_dim = triple // 3
    ff_dev = w_up.shape[1]
    pair = 2 if n_row % 2 == 0 and heads_dev % 2 == 0 and ff_dev % 2 == 0 else 1
    heads = heads_dev // pair
    ff = ff_dev // pair
    joint = heads * triple
    attn = heads * head_dim
    row = lax.axis_index("row")
    col = lax.axis_index("col")
    half = row % pair

    def exchange(halves):
        kept = halves[half]
        given = halves[pair - 1 - half]
        full = jnp.zeros((n_row,) + kept.shape, kept.dtype)
        full = lax.dynamic_update_slice(full, kept[None], (row, 0, 0))
        for offset in range(1, n_row):
            block = lax.ppermute(
                kept if offset % pair == 0 else given, "row", swap(offset, n_row)
            )
            full = lax.dynamic_update_slice(full, block[None], (row ^ offset, 0, 0))
        return full

    def split(w):
        return w.reshape(rows_dev, pair, -1).transpose(1, 0, 2)

    pack_one = jnp.concatenate([split(w_up), split(w_down.T)], axis=2)
    pack_two = jnp.concatenate([split(w_qkv.reshape(rows_dev, -1)), split(w_out.T)], axis=2)
    full_one = exchange(pack_one).reshape(width, 2 * ff)
    full_two = exchange(pack_two).reshape(width, joint + attn)
    w_up_full, w_down_full = full_one[:, :ff], full_one[:, ff:]
    w_qkv_full, w_out_full = full_two[:, :joint], full_two[:, joint:]

    def neighbours(x):
        return [x] + [lax.ppermute(x, "row", swap(1, n_row))] * (pair - 1)

    def gather(x):
        return lax.all_gather(x, "col", axis=1, tiled=True)

    affine = gather(jnp.stack([norm1_gain, norm1_bias, norm2_gain, norm2_bias]))
    token_rows = [gather(x) for x in neighbours(tokens)]
    grad_rows = [gather(x) for x in neighbours(cotangent)]
    docs = neighbours(doc_ids)

    bias_up = lax.dynamic_slice_in_dim(b_up.astype(F32), half * ff, ff)
    bias_qkv = lax.dynamic_slice_in_dim(b_qkv.astype(F32).reshape(-1), half * joint, joint)

    stats = []
    d_joints, d_pres, gelus, attns, outs = [], [], [], [], []
    sum_wd = jnp.zeros((width, ff), F32)
    ones, twos = [], []
    for x, dy, ids in zip(token_rows, grad_rows, docs):
        one, two, stat = normalize(x, affine)
        ones.append(one)
        twos.append(two)
        stats.append(stat)
        pre = jnp.dot(two, w_up_full, preferred_element_type=F32) + bias_up
        gelu, slope = gelu_slope(pre)
        gelu = gelu.astype(BF16)
        d_gelu = jnp.dot(dy, w_down_full, preferred_element_type=F32)
        d_pre = (d_gelu * slope).astype(BF16)
        qkv = jnp.dot(one, w_qkv_full, preferred_element_type=F32) + bias_qkv
        d_attn = jnp.dot(dy, w_out_full, preferred_element_type=F32).astype(BF16)
        starts = run_starts(ids)
        cos, sin = rotary_tables(jnp.arange(seq_rows, dtype=jnp.int32) - starts, head_dim)
        attended, d_joint = attention(qkv, d_attn, starts, cos, sin, head_dim)
        gelus.append(gelu)
        d_pres.append(d_pre)
        attns.append(attended)
        d_joints.append(d_joint)

    def over_tokens(lefts, rights):
        return functools.reduce(
            jnp.add,
            [
                lax.dot_general(a, b, TN, preferred_element_type=F32)
                for a, b in zip(lefts, rights)
            ],
        )

    grad_down = over_tokens(grad_rows, gelus)
    grad_up = over_tokens(twos, d_pres)
    grad_out = over_tokens(grad_rows, attns)
    grad_qkv = over_tokens(ones, d_joints)

    def reduce_rows(partial):
        blocks = partial.reshape(n_row, rows_dev, -1)
        kept = lax.dynamic_index_in_dim(blocks, row, 0, keepdims=False)
        given = None
        for offset in range(1, n_row):
            block = lax.dynamic_index_in_dim(blocks, row ^ offset, 0, keepdims=False)
            block = lax.ppermute(block.astype(BF16), "row", swap(offset, n_row)).astype(F32)
            if offset % pair == 0:
                kept = kept + block
            else:
                given = block if given is None else given + block
        if pair == 1:
            return kept[:, None]
        return jnp.where(
            half == 0, jnp.stack([kept, given], axis=1), jnp.stack([given, kept], axis=1)
        )

    def scatter(parts):
        shares = [
            lax.psum_scatter(p, "col", scatter_dimension=1, tiled=True) for p in parts
        ]
        total = shares[0].astype(F32)
        if pair > 1:
            total = total + lax.ppermute(shares[1], "row", swap(1, n_row)).astype(F32)
        return total

    branch = scatter(
        [
            (
                lax.dot_general(a, w_out_full, NT, preferred_element_type=F32)
                + lax.dot_general(g, w_down_full, NT, preferred_element_type=F32)
            ).astype(BF16)
            for a, g in zip(attns, gelus)
        ]
    )
    affine_wide = affine.astype(F32)
    back = scatter(
        [
            (
                lax.dot_general(dj, w_qkv_full, NT, preferred_element_type=F32) * affine_wide[0]
                + lax.dot_general(dp, w_up_full, NT, preferred_element_type=F32) * affine_wide[2]
            ).astype(BF16)
            for dj, dp in zip(d_joints, d_pres)
        ]
    )

    grad_w_down = reduce_rows(grad_down)
    grad_w_up = reduce_rows(grad_up)
    grad_w_out = reduce_rows(grad_out)
    grad_w_qkv = reduce_rows(grad_qkv)

    sum_joint = functools.reduce(jnp.add, [jnp.sum(d, 0, dtype=F32) for d in d_joints])
    sum_pre = functools.reduce(jnp.add, [jnp.sum(d, 0, dtype=F32) for d in d_pres])
    wide_qkv = w_qkv_full.astype(F32)
    wide_up = w_up_full.astype(F32)
    norm_sums = jnp.stack(
        [
            jnp.sum(wide_qkv * grad_qkv, 1),
            jnp.sum(wide_qkv * sum_joint, 1),
            jnp.sum(wide_up * grad_up, 1),
            jnp.sum(wide_up * sum_pre, 1),
        ]
    )
    norm_sums = lax.psum(norm_sums, ("row", "col"))
    norm_sums = lax.dynamic_slice_in_dim(norm_sums, col * width_dev, width_dev, axis=1)
    gain_one, shift_one = norm1_gain.astype(F32), norm1_bias.astype(F32)
    gain_two, shift_two = norm2_gain.astype(F32), norm2_bias.astype(F32)
    grad_gain_one = (norm_sums[0] - shift_one * norm_sums[1]) / gain_one
    grad_gain_two = (norm_sums[2] - shift_two * norm_sums[3]) / gain_two

    def place(v):
        return lax.dynamic_update_slice(jnp.zeros((pair * v.shape[0],), F32), v, (half * v.shape[0],))

    small = lax.psum(
        jnp.concatenate(
            [place(sum_joint), place(sum_pre), jnp.sum(grad_rows[0], 0, dtype=F32)]
        ),
        "row",
    )
    grad_b_qkv = small[: pair * joint].reshape(heads_dev, triple)
    grad_b_up = small[pair * joint : pair * (joint + ff)]
    grad_b_out = lax.dynamic_slice_in_dim(
        small[pair * (joint + ff) :], row * rows_dev, rows_dev
    )

    bias_out = lax.all_gather(
        jnp.stack([b_out, b_down]), "row", axis=1, tiled=True
    ).astype(F32)
    bias_out = lax.dynamic_slice_in_dim(bias_out[0] + bias_out[1], col * width_dev, width_dev)
    tokens_wide = tokens.astype(F32)
    layer_out = (tokens_wide + bias_out + branch).astype(BF16)

    mean, inv_std = stats[0][:, 0:1], stats[0][:, 1:2]
    normed = (tokens_wide - mean) * inv_std
    sums = lax.psum(jnp.stack([jnp.sum(back, 1), jnp.sum(back * normed, 1)]), "col") / width
    grad_tokens = cotangent.astype(F32) + inv_std * (
        back - sums[0][:, None] - normed * sums[1][:, None]
    )
    return (
        layer_out,
        grad_tokens,
        grad_gain_one,
        norm_sums[1],
        grad_gain_two,
        norm_sums[3],
        grad_w_qkv.reshape(rows_dev, heads_dev, triple),
        grad_b_qkv,
        grad_w_out.reshape(rows_dev, -1).T,
        grad_b_out,
        grad_w_up.reshape(rows_dev, -1),
        grad_b_up,
        grad_w_down.reshape(rows_dev, -1).T,
        grad_b_out,
    )


def solution(mesh):
    placed = (
        P("row", "col"),
        P("row"),
        P("col"),
        P("col"),
        P("col"),
        P("col"),
        P("row", "col", None),
        P("col", None),
        P("col", "row"),
        P("row"),
        P("row", "col"),
        P("col"),
        P("col", "row"),
        P("row"),
        P("row", "col"),
    )
    return jax.shard_map(
        per_device,
        mesh=mesh,
        in_specs=placed,
        out_specs=(
            P("row", "col"),
            P("row", "col"),
            P("col"),
            P("col"),
            P("col"),
            P("col"),
            P("row", "col", None),
            P("col", None),
            P("col", "row"),
            P("row"),
            P("row", "col"),
            P("col"),
            P("col", "row"),
            P("row"),
        ),
        check_vma=False,
    )
```
